512 devices in a mesh: occ: 16 (over x, z_lo), sec: 32 (over z_hi, y, core).
Axes of the slice: x: 4, y: 8, z: 8 (z_hi: 2, z_lo: 4; z = z_hi * 4 + z_lo), core: 2. Of those that a mesh axis runs over, the one named last changes fastest.
Arguments:
- amplitudes: float32 [768, 512, 512], P('occ', None, 'sec'), may hold values from -5 to 5
- live_pairs: int32 [16], replicated, may hold values from 12 to 48, as said below
- ladder_ints: float32 [512, 512, 1024], P('occ', 'sec'), may hold values from -0.0234375 to 0.0234375
- cycle_ints: float32 [48, 512, 6144], P(None, 'sec', 'occ'), may hold values from -0.0390625 to 0.0390625
- pair_ints: float32 [768, 1024], P('occ', 'sec'), may hold values from -6 to 6
- occ_energy: float32 [48], replicated, may hold values from -2 to -0.5
- vir_energy: float32 [512], replicated, may hold values from 0.5 to 4
Outputs:
- new_amplitudes: float32 [768, 1024], P('occ', 'sec')
The draws below stay inside these ranges and needn't reach their ends.
Inputs may be any that keep to these rules, and one draw needn't show every extreme that they name: live_pairs[o] live pairs are the first ones of owner o's 48 pairs; some owner has all of its pairs live.
All inputs are finite; a program needn't handle non-finite values.
Results may differ from the reference program's by a relative error of at most 0.00005.
Values sent between devices are 32-bit elements; how exact they have to be, the bound alone decides.
A program may use at most 64 MiB of HBM per device.

```python
import jax
import jax.numpy as jnp
from jax import lax

OCCUPIED = 48
VIRTUAL = 512
A_WINDOW = 8
B_WINDOW = 128
OWNERS = 16
I_WINDOW = 16
PAIR_OWNER = 48
PAIRS = 768
AB_WINDOW = 1024


def draw_live_pairs(key, part):
    first_key, second_key = jax.random.split(jax.random.fold_in(key, 17))
    counts_drawn = jax.random.randint(first_key, (OWNERS,), max(1, PAIR_OWNER // 4), PAIR_OWNER + 1, dtype=jnp.int32)
    chosen = jax.random.randint(second_key, (), 0, OWNERS, dtype=jnp.int32)
    positions = jnp.arange(OWNERS, dtype=jnp.int32)
    return jnp.where(positions == chosen, PAIR_OWNER, counts_drawn).astype(jnp.int32)


def strengthened(drawn, rng, source, target, parts, factor):
    owner, partner = [(jnp.arange(drawn.shape[position]) // (drawn.shape[position] // parts)).reshape([-1 if axis == position else 1 for axis in range(drawn.ndim)]) for position in (source, target)]
    chosen = jax.random.permutation(rng, parts)[partner]
    strong = (owner == chosen) | (owner == (partner + parts // 2) % parts)
    return jnp.where(strong, factor * drawn, drawn)


def block_scale(own_key, dims, pieces, least, top_value):
    def one(dim, shards_of):
        steps = jax.random.uniform(jax.random.fold_in(jax.random.fold_in(own_key, 6), dim), (shards_of,), jnp.float32, least / len(pieces), top_value / len(pieces))
        return jnp.repeat(jnp.exp(steps), dims[dim] // shards_of).reshape((-1,) + (1,) * (len(dims) - dim - 1))

    level = one(*pieces[0])
    for cut in pieces[1:]:
        level = level * one(*cut)
    return level


def gaussian(own_key, extent, width, reach, cuts=(), held_as=jnp.bfloat16):
    array = width * jax.random.normal(own_key, extent, jnp.float32)
    if cuts:
        array = array * block_scale(own_key, extent, cuts, -0.22, 0.18)
    return jnp.clip(array, -reach, reach).astype(held_as)


def noise_with(stream_key, extent, deviation, most, cuts, heavy, kind=jnp.bfloat16):
    values = deviation * jax.random.normal(stream_key, extent, jnp.float32)
    if cuts:
        values = values * block_scale(stream_key, extent, cuts, -0.22, 0.18)
    return jnp.clip(strengthened(values, jax.random.fold_in(stream_key, 3), *heavy), -most, most).astype(kind)


def setup_inputs(seed: int = 0) -> dict:
    key_list = jax.random.split(jax.random.key(seed), 8)
    amplitudes = gaussian(key_list[0], (PAIRS, VIRTUAL, VIRTUAL), 1.0, 5.0, ((0, 16), (2, 32)), jnp.float32)
    live_pairs = draw_live_pairs(jax.random.fold_in(key_list[7], 71), 0)
    ladder_ints = noise_with(key_list[2], (VIRTUAL, VIRTUAL, AB_WINDOW), (VIRTUAL * VIRTUAL) ** -0.5, 0.0234375, ((0, 16), (1, 32)), (1, 2, 32, 2.75), jnp.float32)
    cycle_ints = gaussian(key_list[3], (OCCUPIED, VIRTUAL, OCCUPIED * B_WINDOW), (OCCUPIED * VIRTUAL) ** -0.5, 0.0390625, ((1, 32), (2, 16)), jnp.float32)
    pair_ints = gaussian(key_list[4], (PAIRS, AB_WINDOW), 1.0, 6.0, ((0, 16), (1, 32)), jnp.float32)
    occ_energy = jnp.clip(jax.random.uniform(key_list[5], (OCCUPIED,), jnp.float32, -2.0, -0.5), -2.0, -0.5)
    vir_energy = jnp.clip(jax.random.uniform(key_list[6], (VIRTUAL,), jnp.float32, 0.5, 4.0), 0.5, 4.0)
    return {"amplitudes": amplitudes, "live_pairs": live_pairs, "ladder_ints": ladder_ints, "cycle_ints": cycle_ints, "pair_ints": pair_ints, "occ_energy": occ_energy, "vir_energy": vir_energy}


highest = lax.Precision.HIGHEST


def reference(amplitudes, live_pairs, ladder_ints, cycle_ints, pair_ints, occ_energy, vir_energy):
    pair_index = jnp.arange(PAIRS, dtype=jnp.int32)
    owner_of = (pair_index // PAIR_OWNER).astype(jnp.int32)
    live_mask = ((pair_index % PAIR_OWNER) < live_pairs[owner_of]).astype(jnp.float32)
    masked = amplitudes * live_mask[:, None, None]
    ladder = jnp.dot(masked.reshape(PAIRS, VIRTUAL * VIRTUAL), ladder_ints.reshape(VIRTUAL * VIRTUAL, AB_WINDOW), precision=highest, preferred_element_type=jnp.float32)
    cycle_rows = masked.reshape(I_WINDOW, OCCUPIED, VIRTUAL, VIRTUAL)[:, :, :A_WINDOW, :]
    cycle_term = jnp.einsum("ikac,kcn->ian", cycle_rows, cycle_ints, precision=highest)
    cycle_term = cycle_term.reshape(I_WINDOW, A_WINDOW, OCCUPIED, B_WINDOW).transpose(0, 2, 1, 3).reshape(PAIRS, AB_WINDOW)
    residual = pair_ints + 0.5 * ladder + cycle_term
    occ_pairs = (occ_energy[:I_WINDOW, None] + occ_energy[None, :]).reshape(PAIRS, 1)
    vir_pairs = (vir_energy[:A_WINDOW, None] + vir_energy[None, :B_WINDOW]).reshape(1, AB_WINDOW)
    return residual / (occ_pairs - vir_pairs) * live_mask[:, None]
```

```python
import jax
import jax.numpy as jnp
from jax import lax
from jax.sharding import PartitionSpec as P

OCCUPIED = 48
VIRTUAL = 512
A_WINDOW = 8
B_WINDOW = 128
I_OWNER = 1


highest = lax.Precision.HIGH


def copy_for_each(array, axis):
    devices = lax.axis_size(axis)
    return lax.all_to_all(
        jnp.broadcast_to(array[None], (devices, *array.shape)), axis, 0, 0, tiled=True
    )


def laid_out(tiles, dim):
    tiles = jnp.moveaxis(tiles, 0, dim)
    lengths = tiles.shape
    return tiles.reshape(*lengths[:dim], lengths[dim] * lengths[dim + 1], *lengths[dim + 2 :])


def gather_directly(array, axis, dim):
    tiles = copy_for_each(array, axis)
    return laid_out(tiles, dim)


def shards(amplitudes, live_pairs, ladder_ints, cycle_ints, pair_ints, occ_energy, vir_energy):
    owners = lax.axis_size("occ")
    sections = lax.axis_size("sec")
    owner_index = lax.axis_index("occ")
    section = lax.axis_index("sec")
    owner_rows = I_OWNER * OCCUPIED
    window_rows = I_OWNER * owners
    owner_cols = OCCUPIED // owners
    col_share = A_WINDOW * B_WINDOW // sections
    d_share = amplitudes.shape[2]
    live_count = lax.dynamic_slice_in_dim(live_pairs, owner_index, 1)[0]
    local_rows = lax.broadcasted_iota(jnp.int32, (owner_rows, 1, 1), 0)
    live_rows = (local_rows < live_count).astype(jnp.float32)
    masked = amplitudes * live_rows
    flat_tiles = masked.reshape(owner_rows, owners, VIRTUAL // owners * d_share)
    regrouped = lax.all_to_all(flat_tiles, "occ", split_axis=1, concat_axis=0, tiled=True)
    pair_total = regrouped.shape[0]
    ladder_part = 0.5 * jnp.dot(
        regrouped.reshape(pair_total, -1),
        ladder_ints.reshape(-1, A_WINDOW * B_WINDOW),
        precision=highest,
        preferred_element_type=jnp.float32,
    )
    cycle_local = masked[:, :A_WINDOW, :].reshape(owner_rows, A_WINDOW * d_share)
    cycle_flat = gather_directly(cycle_local, "occ", 0)
    cycle_rows = cycle_flat.reshape(window_rows, OCCUPIED, A_WINDOW, d_share)
    cycle_part = jnp.einsum(
        "ikac,kcn->ian",
        cycle_rows,
        cycle_ints,
        precision=highest,
        preferred_element_type=jnp.float32,
    )
    cycle_part = (
        cycle_part.reshape(window_rows, A_WINDOW, owner_cols, B_WINDOW)
        .transpose(0, 2, 1, 3)
        .reshape(window_rows, owner_cols, A_WINDOW * B_WINDOW)
    )
    ladder_grid = ladder_part.reshape(window_rows, OCCUPIED, A_WINDOW * B_WINDOW)
    offset = owner_index * owner_cols
    current_part = lax.dynamic_slice_in_dim(ladder_grid, offset, owner_cols, 1)
    ladder_grid = lax.dynamic_update_slice_in_dim(ladder_grid, current_part + cycle_part, offset, 1)
    combined = ladder_grid.reshape(pair_total, A_WINDOW * B_WINDOW)
    first_sum = lax.psum_scatter(combined, "sec", scatter_dimension=1, tiled=True)
    summed = lax.psum_scatter(first_sum, "occ", scatter_dimension=0, tiled=True)
    residual = summed + pair_ints
    occ_rows = lax.dynamic_slice_in_dim(occ_energy, owner_index * I_OWNER, I_OWNER)
    pair_energy = (occ_rows[:, None] + occ_energy[None, :]).reshape(owner_rows, 1)
    vir_pairs = (vir_energy[:A_WINDOW, None] + vir_energy[None, :B_WINDOW]).reshape(
        A_WINDOW * B_WINDOW
    )
    vir_cols = lax.dynamic_slice_in_dim(vir_pairs, section * col_share, col_share)
    denominator = pair_energy - vir_cols[None, :]
    live_out = (lax.broadcasted_iota(jnp.int32, (owner_rows, 1), 0) < live_count).astype(
        jnp.float32
    )
    return residual / denominator * live_out


def solution(mesh):
    in_specs = (
        P("occ", None, "sec"),
        P(),
        P("occ", "sec", None),
        P(None, "sec", "occ"),
        P("occ", "sec"),
        P(),
        P(),
    )
    out_specs = P("occ", "sec")
    return jax.shard_map(shards, mesh=mesh, in_specs=in_specs, out_specs=out_specs, check_vma=False)
```

```python
import jax
import jax.numpy as jnp
from jax import lax
from jax.experimental import pallas as pl
from jax.experimental.pallas import tpu as pltpu
from jax.sharding import PartitionSpec as P

OCCUPIED = 48
VIRTUAL = 512
A_WINDOW = 8
B_WINDOW = 128
X = 4
Z_LOW = 4
Z_HIGH = 2
Y = 8
OWNERS = X * Z_LOW
LANES = 128
C_SHARE = VIRTUAL // OWNERS
D_SHARE = 16
DEPTH = C_SHARE * D_SHARE
J_SHARE = OCCUPIED // OWNERS
COL_SHARE = 32
CHUNKS = ((0, 16), (16, 16), (32, 8), (40, 8))
MESH = pl.DeviceIdType.MESH
F32 = jnp.float32
BF16 = jnp.bfloat16


def halves(value):
    high = value.astype(BF16)
    low = (value - high.astype(F32)).astype(BF16)
    return high, low


def product(left, right):
    (lh, ll), (rh, rl) = left, right
    out = jnp.dot(lh, rl, preferred_element_type=F32)
    out += jnp.dot(ll, rh, preferred_element_type=F32)
    return out + jnp.dot(lh, rh, preferred_element_type=F32)


def settle(ref, sem):
    pltpu.make_async_copy(ref, ref, sem).wait()


def kernel(
    live_ref, occ_ref, vir_ref, t_hbm, w_hbm, u_hbm, pair_ref, out_ref,
    t_v, w_v, u_v, wh, wl, uh, ul, send_t, cyc_own, cyc_all, cyc_out, final, turned,
    local_sem, cyc_sem, t_send, t_recv, core_send, core_recv, y_send, y_recv, p_send, p_recv,
    f_send, f_recv, *bufs,
):
    n = len(CHUNKS)
    recv_t, grid, core_in, y_in, y_out, plane_in = (bufs[k * n : (k + 1) * n] for k in range(6))
    occ = lax.axis_index("occ")
    sec = lax.axis_index("sec")
    x, zl = occ // Z_LOW, occ % Z_LOW
    zh, y, core = sec // 16, (sec // 2) % Y, sec % 2
    half = y % 2
    slot = (occ % 2) * 8 + occ // 2
    holder = jnp.logical_and(zl % 2 == half, zh == core)
    live = live_ref[occ]

    copies = []
    for k in range(X):
        copies.append(
            pltpu.make_async_copy(
                t_hbm.at[:, pl.ds(k * LANES, LANES)], t_v.at[k], local_sem.at[0]
            )
        )
        copies[-1].start()
    for k in range(A_WINDOW):
        pltpu.make_async_copy(
            w_hbm.at[:, pl.ds(k * LANES, LANES)], w_v.at[k], local_sem.at[1]
        ).start()
    pltpu.make_async_copy(u_hbm, u_v, local_sem.at[2]).start()

    barrier = pltpu.get_barrier_semaphore()

    def greet(o, s):
        pl.semaphore_signal(barrier, inc=1, device_id={"occ": o, "sec": s}, device_id_type=MESH)

    def greet_occ(k, carry):
        greet((occ + k) % OWNERS, sec)
        return carry

    def greet_far(k, carry):
        greet((occ + k) % OWNERS, (sec + 16) % 32)
        return carry

    def greet_y(k, carry):
        greet(occ, zh * 16 + ((y + k) % Y) * 2 + core)
        return carry

    lax.fori_loop(1, OWNERS, greet_occ, 0)
    lax.fori_loop(0, OWNERS, greet_far, 0)
    lax.fori_loop(1, Y, greet_y, 0)
    y_twin = y + 1 - 2 * half
    same_y = zh * 16 + y * 2
    twin_y = zh * 16 + y_twin * 2
    greet(occ, same_y + 1 - core)
    greet(occ, twin_y + 1 - core)

    lane_group = lax.broadcasted_iota(jnp.int32, (8, LANES), 1) // C_SHARE
    sub_row = lax.broadcasted_iota(jnp.int32, (8, LANES), 0)

    def relay(r0, rows):
        def tile(k, carry):
            for b in range(rows // 8):
                p0 = r0 + 8 * b
                keep = sub_row + p0 < live
                for g in range(4):
                    part = [
                        jnp.where(keep, t_v[k, pl.ds(p0 * D_SHARE + 4 * g + d, 8, stride=D_SHARE), :], 0.0)
                        for d in range(4)
                    ]
                    for z in range(Z_LOW):
                        row = None
                        for d in range(4):
                            shift = ((d - z) * C_SHARE) % LANES
                            turn = pltpu.roll(part[d], shift, 1) if shift else part[d]
                            row = turn if row is None else jnp.where(lane_group == d, turn, row)
                        send_t[k * Z_LOW + z, p0 : p0 + 8, g * LANES : (g + 1) * LANES] = row
            return carry

        lax.fori_loop(0, X, tile, 0)

    def send_rows(t):
        r0, rows = CHUNKS[t]

        def one(k, carry):
            o = (occ + k) % OWNERS
            pltpu.make_async_remote_copy(
                src_ref=send_t.at[o, pl.ds(r0, rows)],
                dst_ref=recv_t[t].at[slot],
                send_sem=t_send.at[t],
                recv_sem=t_recv.at[t],
                device_id={"occ": o, "sec": sec},
                device_id_type=MESH,
            ).start()
            return carry

        lax.fori_loop(1, OWNERS, one, 0)
        recv_t[t][slot] = send_t[occ, r0 : r0 + rows, :]

    settle(t_v, local_sem.at[0])
    for q in range(OCCUPIED * D_SHARE // LANES):
        rows = lax.broadcasted_iota(jnp.int32, (LANES, LANES), 0) // D_SHARE + q * (LANES // D_SHARE)
        block = jnp.where(rows < live, t_v[0, q * LANES : (q + 1) * LANES, :], 0.0)
        cyc_own[:, q * LANES : (q + 1) * LANES] = block.T[:A_WINDOW, :]
    relay(*CHUNKS[0])
    pl.semaphore_wait(barrier, 40)

    def cyc_z(k, carry):
        pltpu.make_async_remote_copy(
            src_ref=cyc_own,
            dst_ref=cyc_all.at[occ],
            send_sem=cyc_sem.at[0],
            recv_sem=cyc_sem.at[1],
            device_id={"occ": x * Z_LOW + (zl + k) % Z_LOW, "sec": sec},
            device_id_type=MESH,
        ).start()
        return carry

    lax.fori_loop(1, Z_LOW, cyc_z, 0)
    cyc_all[occ] = cyc_own[...]
    send_rows(0)
    relay(*CHUNKS[1])
    send_rows(1)

    settle(cyc_all.at[pl.ds(0, Z_LOW - 1)], cyc_sem.at[1])

    def cyc_x(k, carry):
        mine = cyc_all.at[pl.ds(x * Z_LOW, Z_LOW)]
        pltpu.make_async_remote_copy(
            src_ref=mine,
            dst_ref=mine,
            send_sem=cyc_sem.at[2],
            recv_sem=cyc_sem.at[3],
            device_id={"occ": ((x + k) % X) * Z_LOW + zl, "sec": sec},
            device_id_type=MESH,
        ).start()
        return carry

    lax.fori_loop(1, X, cyc_x, 0)
    for t in range(2, n):
        relay(*CHUNKS[t])

    settle(w_v, local_sem.at[1])

    def weights(a, carry):
        col = pl.multiple_of(((a % 4) * 2 + a // 4) * LANES, LANES)
        for d in range(D_SHARE):
            high, low = halves(w_v[a, pl.ds(d, C_SHARE, stride=D_SHARE), :])
            wh[d * C_SHARE : (d + 1) * C_SHARE, pl.ds(col, LANES)] = high
            wl[d * C_SHARE : (d + 1) * C_SHARE, pl.ds(col, LANES)] = low
        return carry

    lax.fori_loop(0, A_WINDOW, weights, 0)
    settle(u_v, local_sem.at[2])
    for k in range(0, OCCUPIED * D_SHARE, LANES):
        uh[k : k + LANES, :], ul[k : k + LANES, :] = halves(u_v[k : k + LANES, :])

    settle(cyc_all.at[pl.ds(0, OWNERS - Z_LOW)], cyc_sem.at[3])
    settle(cyc_own, cyc_sem.at[0])
    settle(cyc_own, cyc_sem.at[0])
    settle(cyc_own, cyc_sem.at[0])
    settle(cyc_all.at[pl.ds(0, OWNERS - Z_LOW)], cyc_sem.at[2])
    rows_cyc = halves(cyc_all[...].reshape(OWNERS * A_WINDOW, OCCUPIED * D_SHARE))
    cyc = product(rows_cyc, (uh[...], ul[...]))
    for jj in range(J_SHARE):
        cyc_out[jj] = cyc[:, jj * LANES : (jj + 1) * LANES]

    wide = lax.broadcasted_iota(jnp.int32, (COL_SHARE, OCCUPIED), 1)
    tall = lax.broadcasted_iota(jnp.int32, (COL_SHARE, OCCUPIED), 0)
    sub = half * 2 + core
    occ_pair = lax.fori_loop(
        0, OCCUPIED, lambda j, v: jnp.where(wide == j, occ_ref[occ] + occ_ref[j], v),
        jnp.zeros((COL_SHARE, OCCUPIED), F32),
    )
    vir_pair = lax.fori_loop(
        0, COL_SHARE,
        lambda b, v: jnp.where(tall == b, vir_ref[zh * 4 + y // 2] + vir_ref[sub * COL_SHARE + b], v),
        jnp.zeros((COL_SHARE, OCCUPIED), F32),
    )
    bottom = occ_pair - vir_pair
    alive = (wide < live).astype(F32)

    def ladder(t):
        r0, rows = CHUNKS[t]
        left = halves(recv_t[t][...].reshape(OWNERS * rows, DEPTH))
        for al in range(4):
            cols = slice(al * 2 * LANES, (al + 1) * 2 * LANES)
            out = 0.5 * product(left, (wh[:, cols], wl[:, cols]))
            grid[t][0, al] = out[:, :LANES].reshape(2, 8 * rows, LANES)
            grid[t][1, al] = out[:, LANES:].reshape(2, 8 * rows, LANES)
        for jj in range(J_SHARE):
            row = occ * J_SHARE + jj - r0

            @pl.when(jnp.logical_and(row >= 0, row < rows))
            def _():
                for a in range(A_WINDOW):
                    for e in range(2):
                        here = (a // 4, a % 4, e, pl.ds(row, 8, stride=rows), slice(None))
                        grid[t][here] += cyc_out[jj, pl.ds(e * A_WINDOW + a, 8, stride=2 * A_WINDOW), :]

    def core_copy(t):
        return pltpu.make_async_remote_copy(
            src_ref=grid[t].at[1 - core],
            dst_ref=core_in[t],
            send_sem=core_send.at[t],
            recv_sem=core_recv.at[t],
            device_id={"occ": occ, "sec": same_y + 1 - core},
            device_id_type=MESH,
        )

    def along_y(t):
        core_copy(t).wait()
        grid[t][core] += core_in[t][...]

        def one(k, carry):
            to = (y + k) % Y
            pltpu.make_async_remote_copy(
                src_ref=grid[t].at[core, to // 2, to % 2],
                dst_ref=y_in[t].at[y],
                send_sem=y_send.at[t],
                recv_sem=y_recv.at[t],
                device_id={"occ": occ, "sec": zh * 16 + to * 2 + core},
                device_id_type=MESH,
            ).start()
            return carry

        lax.fori_loop(1, Y, one, 0)

    my_pair = occ // 2

    def across_plane(t):
        r0, rows = CHUNKS[t]
        settle(y_in[t].at[pl.ds(0, Y - 1)], y_recv.at[t])
        settle(y_in[t].at[pl.ds(0, Y - 1)], y_send.at[t])
        total = grid[t][core, y // 2, half]
        for k in range(1, Y):
            total += y_in[t][(y + k) % Y]
        y_out[t][...] = total.reshape(8, rows, LANES)

        def one(k, carry):
            @pl.when(jnp.logical_not(jnp.logical_and(holder, k == my_pair)))
            def _():
                pltpu.make_async_remote_copy(
                    src_ref=y_out[t].at[k],
                    dst_ref=plane_in[t].at[zh * OWNERS + occ],
                    send_sem=p_send.at[t],
                    recv_sem=p_recv.at[t],
                    device_id={
                        "occ": (k // 2) * Z_LOW + (k % 2) * 2 + half,
                        "sec": core * 16 + y * 2 + core,
                    },
                    device_id_type=MESH,
                ).start()

            return carry

        lax.fori_loop(0, 8, one, 0)

        @pl.when(holder)
        def _():
            plane_in[t][zh * OWNERS + occ] = y_out[t][my_pair]

    for t in range(n):
        settle(recv_t[t].at[pl.ds(0, OWNERS - 1)], t_recv.at[t])
        if t + 2 < n:
            send_rows(t + 2)
        ladder(t)
        core_copy(t).start()
        if t > 0:
            across_plane(t - 1)
        along_y(t)
    across_plane(n - 1)

    group = (
        {"occ": occ, "sec": same_y + 1 - core},
        {"occ": occ, "sec": twin_y + core},
        {"occ": occ, "sec": twin_y + 1 - core},
    )

    @pl.when(holder)
    def _():
        for t, (r0, rows) in enumerate(CHUNKS):
            settle(plane_in[t].at[pl.ds(0, 31)], p_recv.at[t])
            settle(y_out[t].at[pl.ds(0, 7)], p_send.at[t])
            total = plane_in[t][0]
            for k in range(1, 32):
                total += plane_in[t][k]
            final[r0 : r0 + rows, :] = total
        outs = [
            pltpu.make_async_remote_copy(
                src_ref=final,
                dst_ref=final,
                send_sem=f_send.at[k],
                recv_sem=f_recv,
                device_id=to,
                device_id_type=MESH,
            )
            for k, to in enumerate(group)
        ]
        for copy in outs:
            copy.start()
        for copy in outs:
            copy.wait_send()

    @pl.when(jnp.logical_not(holder))
    def _():
        for t in range(n):
            settle(y_out[t], p_send.at[t])
        settle(final, f_recv)

    turned[...] = final[...].T
    summed = turned[pl.ds(pl.multiple_of(sub * COL_SHARE, COL_SHARE), COL_SHARE), :]
    out_ref[...] = (summed + pair_ref[...]) / bottom * alive

    for t, (r0, rows) in enumerate(CHUNKS):
        settle(send_t.at[pl.ds(0, OWNERS - 1), pl.ds(r0, rows)], t_send.at[t])


def shards(amplitudes, live_pairs, ladder_ints, cycle_ints, pair_ints, occ_energy, vir_energy):
    n = len(CHUNKS)
    smem = pl.BlockSpec(memory_space=pltpu.SMEM)
    vmem = pl.BlockSpec(memory_space=pltpu.VMEM)
    anywhere = pl.BlockSpec(memory_space=pl.ANY)
    dma = pltpu.SemaphoreType.DMA
    rows = [r for _, r in CHUNKS]
    scratch = [
        pltpu.VMEM((X, OCCUPIED * D_SHARE, LANES), F32),
        pltpu.VMEM((A_WINDOW, DEPTH, LANES), F32),
        pltpu.VMEM((OCCUPIED * D_SHARE, J_SHARE * LANES), F32),
        pltpu.VMEM((DEPTH, A_WINDOW * LANES), BF16),
        pltpu.VMEM((DEPTH, A_WINDOW * LANES), BF16),
        pltpu.VMEM((OCCUPIED * D_SHARE, J_SHARE * LANES), BF16),
        pltpu.VMEM((OCCUPIED * D_SHARE, J_SHARE * LANES), BF16),
        pltpu.VMEM((OWNERS, OCCUPIED, DEPTH), F32),
        pltpu.VMEM((A_WINDOW, OCCUPIED * D_SHARE), F32),
        pltpu.VMEM((OWNERS, A_WINDOW, OCCUPIED * D_SHARE), F32),
        pltpu.VMEM((J_SHARE, OWNERS * A_WINDOW, LANES), F32),
        pltpu.VMEM((OCCUPIED, LANES), F32),
        pltpu.VMEM((LANES, OCCUPIED), F32),
        dma((3,)),
        dma((4,)),
        dma((n,)),
        dma((n,)),
        dma((n,)),
        dma((n,)),
        dma((n,)),
        dma((n,)),
        dma((n,)),
        dma((n,)),
        dma((3,)),
        dma,
    ]
    scratch += [pltpu.VMEM((OWNERS, r, DEPTH), F32) for r in rows]
    scratch += [pltpu.VMEM((2, 4, 2, 8 * r, LANES), F32) for r in rows]
    scratch += [pltpu.VMEM((4, 2, 8 * r, LANES), F32) for r in rows]
    scratch += [pltpu.VMEM((Y, 8 * r, LANES), F32) for r in rows]
    scratch += [pltpu.VMEM((8, r, LANES), F32) for r in rows]
    scratch += [pltpu.VMEM((32, r, LANES), F32) for r in rows]
    out = pl.pallas_call(
        kernel,
        out_shape=jax.ShapeDtypeStruct((COL_SHARE, OCCUPIED), F32),
        in_specs=[smem, smem, smem, anywhere, anywhere, anywhere, vmem],
        out_specs=vmem,
        scratch_shapes=scratch,
        compiler_params=pltpu.CompilerParams(
            collective_id=0, has_side_effects=True, vmem_limit_bytes=48 * 1024 * 1024
        ),
    )(
        live_pairs,
        occ_energy,
        vir_energy,
        amplitudes.transpose(0, 2, 1).reshape(OCCUPIED * D_SHARE, VIRTUAL),
        ladder_ints.reshape(DEPTH, A_WINDOW * B_WINDOW),
        cycle_ints.reshape(OCCUPIED * D_SHARE, J_SHARE * B_WINDOW),
        pair_ints.T,
    )
    return out.T


def solution(mesh):
    in_specs = (
        P("occ", None, "sec"),
        P(),
        P("occ", "sec", None),
        P(None, "sec", "occ"),
        P("occ", "sec"),
        P(),
        P(),
    )
    return jax.shard_map(shards, mesh=mesh, in_specs=in_specs, out_specs=P("occ", "sec"), check_vma=False)
```

```python
import jax
import jax.numpy as jnp
from jax import lax
from jax.experimental import pallas as pl
from jax.experimental.pallas import tpu as pltpu
from jax.sharding import PartitionSpec as P

OCCUPIED = 48
VIRTUAL = 512
A_WINDOW = 8
B_WINDOW = 128
X = 4
Z_LOW = 4
Z_HIGH = 2
Y = 8
OWNERS = X * Z_LOW
LANES = 128
C_SHARE = VIRTUAL // OWNERS
D_SHARE = 16
DEPTH = C_SHARE * D_SHARE
J_SHARE = OCCUPIED // OWNERS
COL_SHARE = 32
CHUNKS = tuple((8 * t, 8) for t in range(6))
MESH = pl.DeviceIdType.MESH
F32 = jnp.float32
BF16 = jnp.bfloat16


def halves(value):
    high = value.astype(BF16)
    low = (value - high.astype(F32)).astype(BF16)
    return high, low


def product(left, right):
    (lh, ll), (rh, rl) = left, right
    out = jnp.dot(lh, rl, preferred_element_type=F32)
    out += jnp.dot(ll, rh, preferred_element_type=F32)
    return out + jnp.dot(lh, rh, preferred_element_type=F32)


def settle(ref, sem):
    pltpu.make_async_copy(ref, ref, sem).wait()


def kernel(
    live_hbm, occ_hbm, vir_hbm, t_hbm, w_hbm, u_hbm, pair_hbm, out_ref,
    live_ref, occ_ref, vir_ref, pair_ref, t_v, w_v, u_v, w3, t3, uh, ul, send_t, cyc_own, cyc_all, cyc_out, final, turned,
    local_sem, cyc_sem, t_send, t_recv, core_send, core_recv, y_send, y_mid, y_recv, p_send, p_recv,
    f_send, f_recv, *bufs,
):
    n = len(CHUNKS)
    recv_t, grid, core_in, y_in, y_out, plane_in = (bufs[k * n : (k + 1) * n] for k in range(6))
    occ = lax.axis_index("occ")
    sec = lax.axis_index("sec")
    x, zl = occ // Z_LOW, occ % Z_LOW
    zh, y, core = sec // 16, (sec // 2) % Y, sec % 2
    half = y % 2
    slot = (occ % 2) * 8 + occ // 2
    holder = jnp.logical_and(zl % 2 == half, zh == core)

    live_copy = pltpu.make_async_copy(live_hbm, live_ref, local_sem.at[3])
    live_copy.start()
    for k in range(X):
        pltpu.make_async_copy(
            t_hbm.at[:, pl.ds(k * LANES, LANES)], t_v.at[k], local_sem.at[0]
        ).start()
    for k in range(A_WINDOW):
        pltpu.make_async_copy(
            w_hbm.at[:, pl.ds(k * LANES, LANES)], w_v.at[k], local_sem.at[1]
        ).start()
    pltpu.make_async_copy(u_hbm, u_v, local_sem.at[2]).start()
    small = (
        pltpu.make_async_copy(occ_hbm, occ_ref, local_sem.at[4]),
        pltpu.make_async_copy(vir_hbm, vir_ref, local_sem.at[5]),
        pltpu.make_async_copy(pair_hbm, pair_ref, local_sem.at[6]),
    )
    for copy in small:
        copy.start()

    barrier = pltpu.get_barrier_semaphore()

    def greet(o, s):
        pl.semaphore_signal(barrier, inc=1, device_id={"occ": o, "sec": s}, device_id_type=MESH)

    def greet_occ(k, carry):
        greet((occ + k) % OWNERS, sec)
        return carry

    def greet_far(k, carry):
        greet((occ + k) % OWNERS, (sec + 16) % 32)
        return carry

    def greet_y(k, carry):
        greet(occ, zh * 16 + ((y + k) % Y) * 2 + core)
        return carry

    lax.fori_loop(1, OWNERS, greet_occ, 0)
    lax.fori_loop(0, OWNERS, greet_far, 0)
    lax.fori_loop(1, Y, greet_y, 0)
    y_twin = y + 1 - 2 * half
    same_y = zh * 16 + y * 2
    twin_y = zh * 16 + y_twin * 2
    greet(occ, same_y + 1 - core)
    greet(occ, twin_y + 1 - core)

    lane_group = lax.broadcasted_iota(jnp.int32, (8, LANES), 1) // C_SHARE
    sub_row = lax.broadcasted_iota(jnp.int32, (8, LANES), 0)

    def relay(r0, rows):
        def tile(k, carry):
            for b in range(rows // 8):
                p0 = r0 + 8 * b
                keep = sub_row + p0 < live
                for g in range(4):
                    part = [
                        jnp.where(keep, t_v[k, pl.ds(p0 * D_SHARE + 4 * g + d, 8, stride=D_SHARE), :], 0.0)
                        for d in range(4)
                    ]
                    for z in range(Z_LOW):
                        row = None
                        for d in range(4):
                            shift = ((d - z) * C_SHARE) % LANES
                            turn = pltpu.roll(part[d], shift, 1) if shift else part[d]
                            row = turn if row is None else jnp.where(lane_group == d, turn, row)
                        send_t[k * Z_LOW + z, p0 : p0 + 8, g * LANES : (g + 1) * LANES] = row
            return carry

        lax.fori_loop(0, X, tile, 0)

    def send_rows(t):
        r0, rows = CHUNKS[t]

        def one(k, carry):
            o = (occ + k) % OWNERS
            pltpu.make_async_remote_copy(
                src_ref=send_t.at[o, pl.ds(r0, rows)],
                dst_ref=recv_t[t].at[slot],
                send_sem=t_send.at[t],
                recv_sem=t_recv.at[t],
                device_id={"occ": o, "sec": sec},
                device_id_type=MESH,
            ).start()
            return carry

        lax.fori_loop(1, OWNERS, one, 0)
        recv_t[t][slot] = send_t[occ, r0 : r0 + rows, :]

    live_copy.wait()
    live = live_ref[occ]
    settle(t_v, local_sem.at[0])
    for q in range(OCCUPIED * D_SHARE // LANES):
        rows = lax.broadcasted_iota(jnp.int32, (LANES, LANES), 0) // D_SHARE + q * (LANES // D_SHARE)
        block = jnp.where(rows < live, t_v[0, q * LANES : (q + 1) * LANES, :], 0.0)
        cyc_own[:, q * LANES : (q + 1) * LANES] = block.T[:A_WINDOW, :]
    relay(*CHUNKS[0])
    pl.semaphore_wait(barrier, 40)

    def cyc_z(k, carry):
        pltpu.make_async_remote_copy(
            src_ref=cyc_own,
            dst_ref=cyc_all.at[occ],
            send_sem=cyc_sem.at[0],
            recv_sem=cyc_sem.at[1],
            device_id={"occ": x * Z_LOW + (zl + k) % Z_LOW, "sec": sec},
            device_id_type=MESH,
        ).start()
        return carry

    lax.fori_loop(1, Z_LOW, cyc_z, 0)
    cyc_all[occ] = cyc_own[...]
    send_rows(0)
    relay(*CHUNKS[1])
    send_rows(1)

    settle(cyc_all.at[pl.ds(0, Z_LOW - 1)], cyc_sem.at[1])

    def cyc_x(k, carry):
        mine = cyc_all.at[pl.ds(x * Z_LOW, Z_LOW)]
        pltpu.make_async_remote_copy(
            src_ref=mine,
            dst_ref=mine,
            send_sem=cyc_sem.at[2],
            recv_sem=cyc_sem.at[3],
            device_id={"occ": ((x + k) % X) * Z_LOW + zl, "sec": sec},
            device_id_type=MESH,
        ).start()
        return carry

    lax.fori_loop(1, X, cyc_x, 0)
    for t in range(2, n):
        relay(*CHUNKS[t])
        send_rows(t)

    settle(w_v, local_sem.at[1])

    def weights(a, carry):
        col = pl.multiple_of(((a % 4) * 2 + a // 4) * LANES, LANES)
        for d in range(D_SHARE):
            high, low = halves(w_v[a, pl.ds(d, C_SHARE, stride=D_SHARE), :])
            for k, half_of in enumerate((low, high, high)):
                w3[k * DEPTH + d * C_SHARE : k * DEPTH + (d + 1) * C_SHARE, pl.ds(col, LANES)] = half_of
        return carry

    lax.fori_loop(0, A_WINDOW, weights, 0)
    settle(u_v, local_sem.at[2])
    for k in range(0, OCCUPIED * D_SHARE, LANES):
        uh[k : k + LANES, :], ul[k : k + LANES, :] = halves(u_v[k : k + LANES, :])

    settle(cyc_all.at[pl.ds(0, OWNERS - Z_LOW)], cyc_sem.at[3])
    settle(cyc_all.at[pl.ds(0, Z_LOW - 1)], cyc_sem.at[0])
    settle(cyc_all.at[pl.ds(0, OWNERS - Z_LOW)], cyc_sem.at[2])
    rows_cyc = halves(cyc_all[...].reshape(OWNERS * A_WINDOW, OCCUPIED * D_SHARE))
    cyc = product(rows_cyc, (uh[...], ul[...]))
    for jj in range(J_SHARE):
        cyc_out[jj] = cyc[:, jj * LANES : (jj + 1) * LANES]

    for copy in small:
        copy.wait()
    wide = lax.broadcasted_iota(jnp.int32, (COL_SHARE, OCCUPIED), 1)
    tall = lax.broadcasted_iota(jnp.int32, (COL_SHARE, OCCUPIED), 0)
    sub = half * 2 + core
    occ_pair = lax.fori_loop(
        0, OCCUPIED, lambda j, v: jnp.where(wide == j, occ_ref[occ] + occ_ref[j], v),
        jnp.zeros((COL_SHARE, OCCUPIED), F32),
    )
    vir_pair = lax.fori_loop(
        0, COL_SHARE,
        lambda b, v: jnp.where(tall == b, vir_ref[zh * 4 + y // 2] + vir_ref[sub * COL_SHARE + b], v),
        jnp.zeros((COL_SHARE, OCCUPIED), F32),
    )
    bottom = occ_pair - vir_pair
    alive = (wide < live).astype(F32)

    def core_piece(t, al):
        return pltpu.make_async_remote_copy(
            src_ref=grid[t].at[1 - core, al],
            dst_ref=core_in[t].at[al],
            send_sem=core_send.at[t],
            recv_sem=core_recv.at[t],
            device_id={"occ": occ, "sec": same_y + 1 - core},
            device_id_type=MESH,
        )

    def ladder(t):
        settle(recv_t[t].at[pl.ds(0, OWNERS - 1)], t_recv.at[t])
        r0, rows = CHUNKS[t]
        high, low = halves(recv_t[t][...].reshape(OWNERS * rows, DEPTH))
        left = t3.at[pl.ds(0, OWNERS * rows)]
        left[:, :DEPTH] = high
        left[:, DEPTH : 2 * DEPTH] = low
        left[:, 2 * DEPTH :] = high
        for al in range(4):
            cols = slice(al * 2 * LANES, (al + 1) * 2 * LANES)
            out = 0.5 * jnp.dot(left[...], w3[:, cols], preferred_element_type=F32)
            grid[t][0, al] = out[:, :LANES].reshape(2, 8 * rows, LANES)
            grid[t][1, al] = out[:, LANES:].reshape(2, 8 * rows, LANES)
            for jj in range(J_SHARE):
                row = occ * J_SHARE + jj - r0

                @pl.when(jnp.logical_and(row >= 0, row < rows))
                def _():
                    for ah in range(2):
                        for e in range(2):
                            here = (ah, al, e, pl.ds(row, 8, stride=rows), slice(None))
                            a = ah * 4 + al
                            grid[t][here] += cyc_out[jj, pl.ds(e * A_WINDOW + a, 8, stride=2 * A_WINDOW), :]

            core_piece(t, al).start()

    def ship(src, dst, send, recv, to):
        pltpu.make_async_remote_copy(
            src_ref=src,
            dst_ref=dst,
            send_sem=send,
            recv_sem=recv,
            device_id={"occ": occ, "sec": zh * 16 + to * 2 + core},
            device_id_type=MESH,
        ).start()

    def portion(t, to):
        return grid[t].at[core, to // 2, to % 2]

    steps = ((0, 1), (1, Y - 1))

    def first_round(t):
        settle(core_in[t], core_recv.at[t])
        grid[t][core] += core_in[t][...]
        part = 4 * CHUNKS[t][1]
        for d, step in steps:
            ship(
                portion(t, (y + 3 * step) % Y), y_in[t].at[pl.ds(d * 2 * part, 2 * part)],
                y_send.at[t], y_mid.at[t], (y + step) % Y,
            )
            ship(
                portion(t, (y + 4) % Y).at[pl.ds(d * part, part)], y_in[t].at[pl.ds((4 + d) * part, part)],
                y_send.at[t], y_mid.at[t], (y + 2 * step) % Y,
            )
        for d, step in steps:
            ship(
                portion(t, (y + step) % Y), y_in[t].at[pl.ds((6 + 2 * d) * part, 2 * part)],
                y_send.at[t], y_recv.at[t], (y + step) % Y,
            )

    def second_round(t):
        part = 4 * CHUNKS[t][1]
        settle(y_in[t].at[pl.ds(0, 6 * part)], y_mid.at[t])
        for d, step in steps:
            to = (y + 2 * step) % Y
            whole = portion(t, to)
            whole[...] += y_in[t][d * 2 * part : (d + 1) * 2 * part, :]
            whole[d * part : (d + 1) * part, :] += y_in[t][(4 + d) * part : (5 + d) * part, :]
            ship(
                whole, y_in[t].at[pl.ds((10 + 2 * d) * part, 2 * part)],
                y_send.at[t], y_recv.at[t], to,
            )

    my_pair = occ // 2

    def across_plane(t):
        r0, rows = CHUNKS[t]
        part = 4 * rows
        settle(y_in[t].at[pl.ds(6 * part, 8 * part)], y_recv.at[t])
        total = grid[t][core, y // 2, half]
        for k in range(4):
            total += y_in[t][(6 + 2 * k) * part : (8 + 2 * k) * part, :]
        y_out[t][...] = total.reshape(8, rows, LANES)

        def one(k, carry):
            @pl.when(jnp.logical_not(jnp.logical_and(holder, k == my_pair)))
            def _():
                pltpu.make_async_remote_copy(
                    src_ref=y_out[t].at[k],
                    dst_ref=plane_in[t].at[zh * OWNERS + occ],
                    send_sem=p_send.at[t],
                    recv_sem=p_recv.at[t],
                    device_id={
                        "occ": (k // 2) * Z_LOW + (k % 2) * 2 + half,
                        "sec": core * 16 + y * 2 + core,
                    },
                    device_id_type=MESH,
                ).start()

            return carry

        lax.fori_loop(0, 8, one, 0)

        @pl.when(holder)
        def _():
            plane_in[t][zh * OWNERS + occ] = y_out[t][my_pair]

    for t in range(n + 2):
        if t < n:
            ladder(t)
        if 1 <= t <= n:
            second_round(t - 1)
        if t >= 2:
            across_plane(t - 2)
        if t < n:
            first_round(t)

    group = (
        {"occ": occ, "sec": same_y + 1 - core},
        {"occ": occ, "sec": twin_y + core},
        {"occ": occ, "sec": twin_y + 1 - core},
    )

    @pl.when(holder)
    def _():
        for t, (r0, rows) in enumerate(CHUNKS):
            settle(plane_in[t].at[pl.ds(0, 31)], p_recv.at[t])
            settle(y_out[t].at[pl.ds(0, 7)], p_send.at[t])
            total = plane_in[t][0]
            for k in range(1, 32):
                total += plane_in[t][k]
            final[r0 : r0 + rows, :] = total
        outs = [
            pltpu.make_async_remote_copy(
                src_ref=final,
                dst_ref=final,
                send_sem=f_send.at[k],
                recv_sem=f_recv,
                device_id=to,
                device_id_type=MESH,
            )
            for k, to in enumerate(group)
        ]
        for copy in outs:
            copy.start()
        for copy in outs:
            copy.wait_send()

    @pl.when(jnp.logical_not(holder))
    def _():
        for t in range(n):
            settle(y_out[t], p_send.at[t])
        settle(final, f_recv)

    turned[...] = final[...].T
    summed = turned[pl.ds(pl.multiple_of(sub * COL_SHARE, COL_SHARE), COL_SHARE), :]
    out_ref[...] = (summed + pair_ref[...]) / bottom * alive

    for t, (r0, rows) in enumerate(CHUNKS):
        settle(send_t.at[pl.ds(0, OWNERS - 1), pl.ds(r0, rows)], t_send.at[t])
        settle(core_in[t], core_send.at[t])
        settle(y_in[t], y_send.at[t])


def shards(amplitudes, live_pairs, ladder_ints, cycle_ints, pair_ints, occ_energy, vir_energy):
    n = len(CHUNKS)
    vmem = pl.BlockSpec(memory_space=pltpu.VMEM)
    hbm = pl.BlockSpec(memory_space=pltpu.HBM)
    dma = pltpu.SemaphoreType.DMA
    rows = [r for _, r in CHUNKS]
    scratch = [
        pltpu.SMEM((OWNERS,), jnp.int32),
        pltpu.SMEM((OCCUPIED,), F32),
        pltpu.SMEM((VIRTUAL,), F32),
        pltpu.VMEM((COL_SHARE, OCCUPIED), F32),
        pltpu.VMEM((X, OCCUPIED * D_SHARE, LANES), F32),
        pltpu.VMEM((A_WINDOW, DEPTH, LANES), F32),
        pltpu.VMEM((OCCUPIED * D_SHARE, J_SHARE * LANES), F32),
        pltpu.VMEM((3 * DEPTH, A_WINDOW * LANES), BF16),
        pltpu.VMEM((OWNERS * max(rows), 3 * DEPTH), BF16),
        pltpu.VMEM((OCCUPIED * D_SHARE, J_SHARE * LANES), BF16),
        pltpu.VMEM((OCCUPIED * D_SHARE, J_SHARE * LANES), BF16),
        pltpu.VMEM((OWNERS, OCCUPIED, DEPTH), F32),
        pltpu.VMEM((A_WINDOW, OCCUPIED * D_SHARE), F32),
        pltpu.VMEM((OWNERS, A_WINDOW, OCCUPIED * D_SHARE), F32),
        pltpu.VMEM((J_SHARE, OWNERS * A_WINDOW, LANES), F32),
        pltpu.VMEM((OCCUPIED, LANES), F32),
        pltpu.VMEM((LANES, OCCUPIED), F32),
        dma((7,)),
        dma((4,)),
        dma((n,)),
        dma((n,)),
        dma((n,)),
        dma((n,)),
        dma((n,)),
        dma((n,)),
        dma((n,)),
        dma((n,)),
        dma((n,)),
        dma((3,)),
        dma,
    ]
    scratch += [pltpu.VMEM((OWNERS, r, DEPTH), F32) for r in rows]
    scratch += [pltpu.VMEM((2, 4, 2, 8 * r, LANES), F32) for r in rows]
    scratch += [pltpu.VMEM((4, 2, 8 * r, LANES), F32) for r in rows]
    scratch += [pltpu.VMEM((56 * r, LANES), F32) for r in rows]
    scratch += [pltpu.VMEM((8, r, LANES), F32) for r in rows]
    scratch += [pltpu.VMEM((32, r, LANES), F32) for r in rows]
    out = pl.pallas_call(
        kernel,
        out_shape=jax.ShapeDtypeStruct((COL_SHARE, OCCUPIED), F32),
        in_specs=[hbm] * 7,
        out_specs=vmem,
        scratch_shapes=scratch,
        compiler_params=pltpu.CompilerParams(
            collective_id=0, has_side_effects=True, vmem_limit_bytes=48 * 1024 * 1024
        ),
    )(
        *(
            pltpu.with_memory_space_constraint(array, pltpu.HBM)
            for array in (
                live_pairs,
                occ_energy,
                vir_energy,
                amplitudes.transpose(0, 2, 1).reshape(OCCUPIED * D_SHARE, VIRTUAL),
                ladder_ints.reshape(DEPTH, A_WINDOW * B_WINDOW),
                cycle_ints.reshape(OCCUPIED * D_SHARE, J_SHARE * B_WINDOW),
                pair_ints.T,
            )
        )
    )
    return out.T


def solution(mesh):
    in_specs = (
        P("occ", None, "sec"),
        P(),
        P("occ", "sec", None),
        P(None, "sec", "occ"),
        P("occ", "sec"),
        P(),
        P(),
    )
    return jax.shard_map(shards, mesh=mesh, in_specs=in_specs, out_specs=P("occ", "sec"), check_vma=False)
```

```python
import jax
import jax.numpy as jnp
from jax import lax
from jax.experimental import pallas as pl
from jax.experimental.pallas import tpu as pltpu
from jax.sharding import PartitionSpec as P

OCCUPIED = 48
VIRTUAL = 512
A_WINDOW = 8
B_WINDOW = 128
X = 4
Z_LOW = 4
Z_HIGH = 2
Y = 8
OWNERS = X * Z_LOW
LANES = 128
C_SHARE = VIRTUAL // OWNERS
D_SHARE = 16
DEPTH = C_SHARE * D_SHARE
J_SHARE = OCCUPIED // OWNERS
COL_SHARE = 32
CHUNKS = tuple((8 * t, 8) for t in range(6))
AHEAD = 3
MESH = pl.DeviceIdType.MESH
F32 = jnp.float32
BF16 = jnp.bfloat16


def halves(value):
    high = value.astype(BF16)
    low = (value - high.astype(F32)).astype(BF16)
    return high, low


def product(left, right):
    (lh, ll), (rh, rl) = left, right
    out = jnp.dot(lh, rl, preferred_element_type=F32)
    out += jnp.dot(ll, rh, preferred_element_type=F32)
    return out + jnp.dot(lh, rh, preferred_element_type=F32)


def settle(ref, sem):
    pltpu.make_async_copy(ref, ref, sem).wait()


def kernel(
    live_hbm, occ_hbm, vir_hbm, t_hbm, w_hbm, u_hbm, pair_hbm, out_ref,
    live_ref, occ_ref, vir_ref, pair_ref, t_v, w_v, u_v, w3, t3, uh, ul, send_t, cyc_own, cyc_all, cyc_out, final, turned, bottom,
    local_sem, cyc_sem, t_send, t_recv, core_send, core_recv, y_send, y_mid, y_recv, x_send, x_recv, p_send, p_recv,
    f_send, f_recv, *bufs,
):
    n = len(CHUNKS)
    recv_t, grid, core_in, y_in, y_out, x_in, x_out, plane_in = (
        bufs[k * n : (k + 1) * n] for k in range(8)
    )
    occ = lax.axis_index("occ")
    sec = lax.axis_index("sec")
    x, zl = occ // Z_LOW, occ % Z_LOW
    zh, y, core = sec // 16, (sec // 2) % Y, sec % 2
    half = y % 2
    slot = (occ % 2) * 8 + occ // 2
    holder = jnp.logical_and(zl % 2 == half, zh == core)

    live_copy = pltpu.make_async_copy(live_hbm, live_ref, local_sem.at[3])
    live_copy.start()
    early = CHUNKS[0][1] * D_SHARE
    late = OCCUPIED * D_SHARE - early
    for part, (at, size) in enumerate(((0, early), (early, late))):
        for k in range(X):
            pltpu.make_async_copy(
                t_hbm.at[pl.ds(at, size), pl.ds(k * LANES, LANES)],
                t_v.at[k, pl.ds(at, size)],
                local_sem.at[7 * part],
            ).start()
    for k in range(A_WINDOW):
        pltpu.make_async_copy(
            w_hbm.at[:, pl.ds(k * LANES, LANES)], w_v.at[k], local_sem.at[1]
        ).start()
    pltpu.make_async_copy(u_hbm, u_v, local_sem.at[2]).start()
    small = (
        pltpu.make_async_copy(occ_hbm, occ_ref, local_sem.at[4]),
        pltpu.make_async_copy(vir_hbm, vir_ref, local_sem.at[5]),
        pltpu.make_async_copy(pair_hbm, pair_ref, local_sem.at[6]),
    )
    for copy in small:
        copy.start()

    barrier = pltpu.get_barrier_semaphore()

    def greet(o, s):
        pl.semaphore_signal(barrier, inc=1, device_id={"occ": o, "sec": s}, device_id_type=MESH)

    def greet_occ(k, carry):
        greet((occ + k) % OWNERS, sec)
        return carry

    def greet_far(k, carry):
        greet(x * Z_LOW + k, (sec + 16) % 32)
        return carry

    def greet_y(k, carry):
        greet(occ, zh * 16 + ((y + k) % Y) * 2 + core)
        return carry

    lax.fori_loop(1, OWNERS, greet_occ, 0)
    lax.fori_loop(0, Z_LOW, greet_far, 0)
    lax.fori_loop(1, Y, greet_y, 0)
    y_twin = y + 1 - 2 * half
    same_y = zh * 16 + y * 2
    twin_y = zh * 16 + y_twin * 2
    greet(occ, same_y + 1 - core)
    greet(occ, twin_y + 1 - core)

    lane_group = lax.broadcasted_iota(jnp.int32, (8, LANES), 1) // C_SHARE
    sub_row = lax.broadcasted_iota(jnp.int32, (8, LANES), 0)

    def relay(r0, rows):
        def tile(k, carry):
            for b in range(rows // 8):
                p0 = r0 + 8 * b
                keep = sub_row + p0 < live
                for g in range(4):
                    part = [
                        jnp.where(keep, t_v[k, pl.ds(p0 * D_SHARE + 4 * g + d, 8, stride=D_SHARE), :], 0.0)
                        for d in range(4)
                    ]
                    for z in range(Z_LOW):
                        row = None
                        for d in range(4):
                            shift = ((d - z) * C_SHARE) % LANES
                            turn = pltpu.roll(part[d], shift, 1) if shift else part[d]
                            row = turn if row is None else jnp.where(lane_group == d, turn, row)
                        send_t[k * Z_LOW + z, p0 : p0 + 8, g * LANES : (g + 1) * LANES] = row
            return carry

        lax.fori_loop(0, X, tile, 0)

    def send_rows(t):
        r0, rows = CHUNKS[t]

        def one(k, carry):
            o = (occ + k) % OWNERS
            pltpu.make_async_remote_copy(
                src_ref=send_t.at[o, pl.ds(r0, rows)],
                dst_ref=recv_t[t].at[slot],
                send_sem=t_send.at[t],
                recv_sem=t_recv.at[t],
                device_id={"occ": o, "sec": sec},
                device_id_type=MESH,
            ).start()
            return carry

        lax.fori_loop(1, OWNERS, one, 0)
        recv_t[t][slot] = send_t[occ, r0 : r0 + rows, :]

    live_copy.wait()
    live = live_ref[occ]
    settle(t_v.at[:, pl.ds(0, early)], local_sem.at[0])
    relay(*CHUNKS[0])
    pl.semaphore_wait(barrier, 28)
    send_rows(0)
    settle(t_v.at[:, pl.ds(early, late)], local_sem.at[7])
    for q in range(OCCUPIED * D_SHARE // LANES):
        rows = lax.broadcasted_iota(jnp.int32, (LANES, LANES), 0) // D_SHARE + q * (LANES // D_SHARE)
        block = jnp.where(rows < live, t_v[0, q * LANES : (q + 1) * LANES, :], 0.0)
        cyc_own[:, q * LANES : (q + 1) * LANES] = block.T[:A_WINDOW, :]

    def cyc_z(k, carry):
        pltpu.make_async_remote_copy(
            src_ref=cyc_own,
            dst_ref=cyc_all.at[occ],
            send_sem=cyc_sem.at[0],
            recv_sem=cyc_sem.at[1],
            device_id={"occ": x * Z_LOW + (zl + k) % Z_LOW, "sec": sec},
            device_id_type=MESH,
        ).start()
        return carry

    lax.fori_loop(1, Z_LOW, cyc_z, 0)
    cyc_all[occ] = cyc_own[...]
    for t in range(1, AHEAD):
        relay(*CHUNKS[t])
        send_rows(t)

    settle(cyc_all.at[pl.ds(0, Z_LOW - 1)], cyc_sem.at[1])

    def cyc_x(k, carry):
        mine = cyc_all.at[pl.ds(x * Z_LOW, Z_LOW)]
        pltpu.make_async_remote_copy(
            src_ref=mine,
            dst_ref=mine,
            send_sem=cyc_sem.at[2],
            recv_sem=cyc_sem.at[3],
            device_id={"occ": ((x + k) % X) * Z_LOW + zl, "sec": sec},
            device_id_type=MESH,
        ).start()
        return carry

    lax.fori_loop(1, X, cyc_x, 0)
    settle(w_v, local_sem.at[1])

    def weights(a, carry):
        col = pl.multiple_of(((a % 4) * 2 + a // 4) * LANES, LANES)
        for d in range(D_SHARE):
            high, low = halves(w_v[a, pl.ds(d, C_SHARE, stride=D_SHARE), :])
            for k, half_of in enumerate((low, high, high)):
                w3[k * DEPTH + d * C_SHARE : k * DEPTH + (d + 1) * C_SHARE, pl.ds(col, LANES)] = half_of
        return carry

    lax.fori_loop(0, A_WINDOW, weights, 0)
    settle(u_v, local_sem.at[2])
    for k in range(0, OCCUPIED * D_SHARE, LANES):
        uh[k : k + LANES, :], ul[k : k + LANES, :] = halves(u_v[k : k + LANES, :])

    settle(cyc_all.at[pl.ds(0, OWNERS - Z_LOW)], cyc_sem.at[3])
    settle(cyc_all.at[pl.ds(0, Z_LOW - 1)], cyc_sem.at[0])
    settle(cyc_all.at[pl.ds(0, OWNERS - Z_LOW)], cyc_sem.at[2])
    rows_cyc = halves(cyc_all[...].reshape(OWNERS * A_WINDOW, OCCUPIED * D_SHARE))
    cyc = product(rows_cyc, (uh[...], ul[...]))
    for jj in range(J_SHARE):
        cyc_out[jj] = cyc[:, jj * LANES : (jj + 1) * LANES]

    wide = lax.broadcasted_iota(jnp.int32, (COL_SHARE, OCCUPIED), 1)
    tall = lax.broadcasted_iota(jnp.int32, (COL_SHARE, OCCUPIED), 0)
    sub = half * 2 + core

    def denominators():
        for copy in small:
            copy.wait()
        occ_pair = lax.fori_loop(
            0, OCCUPIED, lambda j, v: jnp.where(wide == j, occ_ref[occ] + occ_ref[j], v),
            jnp.zeros((COL_SHARE, OCCUPIED), F32),
        )
        vir_pair = lax.fori_loop(
            0, COL_SHARE,
            lambda b, v: jnp.where(tall == b, vir_ref[zh * 4 + y // 2] + vir_ref[sub * COL_SHARE + b], v),
            jnp.zeros((COL_SHARE, OCCUPIED), F32),
        )
        bottom[...] = occ_pair - vir_pair

    def core_piece(t, al):
        return pltpu.make_async_remote_copy(
            src_ref=grid[t].at[1 - core, al],
            dst_ref=core_in[t].at[al],
            send_sem=core_send.at[t],
            recv_sem=core_recv.at[t],
            device_id={"occ": occ, "sec": same_y + 1 - core},
            device_id_type=MESH,
        )

    def ladder(t):
        settle(recv_t[t].at[pl.ds(0, OWNERS - 1)], t_recv.at[t])
        r0, rows = CHUNKS[t]
        if t + AHEAD < n:
            relay(*CHUNKS[t + AHEAD])
            send_rows(t + AHEAD)
        high, low = halves(recv_t[t][...].reshape(OWNERS * rows, DEPTH))
        left = t3.at[pl.ds(0, OWNERS * rows)]
        left[:, :DEPTH] = high
        left[:, DEPTH : 2 * DEPTH] = low
        left[:, 2 * DEPTH :] = high
        for al in range(4):
            if al % 2 == 0:
                cols = slice(al * 2 * LANES, (al + 2) * 2 * LANES)
                out = 0.5 * jnp.dot(left[...], w3[:, cols], preferred_element_type=F32)
                for q in range(4):
                    piece = out[:, q * LANES : (q + 1) * LANES]
                    grid[t][q % 2, al + q // 2] = piece.reshape(2, 8 * rows, LANES)
            for jj in range(J_SHARE):
                row = occ * J_SHARE + jj - r0

                @pl.when(jnp.logical_and(row >= 0, row < rows))
                def _():
                    for ah in range(2):
                        for e in range(2):
                            here = (ah, al, e, pl.ds(row, 8, stride=rows), slice(None))
                            a = ah * 4 + al
                            grid[t][here] += cyc_out[jj, pl.ds(e * A_WINDOW + a, 8, stride=2 * A_WINDOW), :]

            core_piece(t, al).start()

    def ship(src, dst, send, recv, to):
        pltpu.make_async_remote_copy(
            src_ref=src,
            dst_ref=dst,
            send_sem=send,
            recv_sem=recv,
            device_id={"occ": occ, "sec": zh * 16 + to * 2 + core},
            device_id_type=MESH,
        ).start()

    def portion(t, to):
        return grid[t].at[core, to // 2, to % 2]

    steps = ((0, 1), (1, Y - 1))

    def first_round(t):
        settle(core_in[t], core_recv.at[t])
        grid[t][core] += core_in[t][...]
        part = 4 * CHUNKS[t][1]
        for d, step in steps:
            ship(
                portion(t, (y + 3 * step) % Y), y_in[t].at[pl.ds(d * 2 * part, 2 * part)],
                y_send.at[t], y_mid.at[t], (y + step) % Y,
            )
            ship(
                portion(t, (y + 4) % Y).at[pl.ds(d * part, part)], y_in[t].at[pl.ds((4 + d) * part, part)],
                y_send.at[t], y_mid.at[t], (y + 2 * step) % Y,
            )
        for d, step in steps:
            ship(
                portion(t, (y + step) % Y), y_in[t].at[pl.ds((6 + 2 * d) * part, 2 * part)],
                y_send.at[t], y_recv.at[t], (y + step) % Y,
            )

    def second_round(t):
        part = 4 * CHUNKS[t][1]
        settle(y_in[t].at[pl.ds(0, 6 * part)], y_mid.at[t])
        for d, step in steps:
            to = (y + 2 * step) % Y
            whole = portion(t, to)
            whole[...] += y_in[t][d * 2 * part : (d + 1) * 2 * part, :]
            whole[d * part : (d + 1) * part, :] += y_in[t][(4 + d) * part : (5 + d) * part, :]
            ship(
                whole, y_in[t].at[pl.ds((10 + 2 * d) * part, 2 * part)],
                y_send.at[t], y_recv.at[t], to,
            )

    def along_x(t):
        r0, rows = CHUNKS[t]
        part = 4 * rows
        settle(y_in[t].at[pl.ds(6 * part, 8 * part)], y_recv.at[t])
        total = grid[t][core, y // 2, half]
        for k in range(4):
            total += y_in[t][(6 + 2 * k) * part : (8 + 2 * k) * part, :]
        y_out[t][...] = total.reshape(8, rows, LANES)

        for k in range(1, X):
            to = (x + k) % X
            pltpu.make_async_remote_copy(
                src_ref=y_out[t].at[pl.ds(2 * to, 2)],
                dst_ref=x_in[t].at[k - 1],
                send_sem=x_send.at[t],
                recv_sem=x_recv.at[t],
                device_id={"occ": to * Z_LOW + zl, "sec": sec},
                device_id_type=MESH,
            ).start()

    def along_z(t):
        settle(x_in[t], x_recv.at[t])
        total = y_out[t][pl.ds(2 * x, 2)]
        for k in range(X - 1):
            total += x_in[t][k]
        x_out[t][...] = total
        for k in range(2):
            mine = jnp.logical_and(holder, zl // 2 == k)

            @pl.when(jnp.logical_not(mine))
            def _():
                pltpu.make_async_remote_copy(
                    src_ref=x_out[t].at[k],
                    dst_ref=plane_in[t].at[zh * Z_LOW + zl],
                    send_sem=p_send.at[t],
                    recv_sem=p_recv.at[t],
                    device_id={"occ": x * Z_LOW + 2 * k + half, "sec": core * 16 + y * 2 + core},
                    device_id_type=MESH,
                ).start()

            @pl.when(mine)
            def _():
                plane_in[t][zh * Z_LOW + zl] = x_out[t][k]

    for t in range(n + 4):
        if t < n:
            ladder(t)
            first_round(t)
        if 0 <= t - 4:
            along_z(t - 4)
        if 0 <= t - 3 < n:
            along_x(t - 3)
        if 0 <= t - 1 < n:
            second_round(t - 1)
        if t == 0:
            denominators()

    group = (
        {"occ": occ, "sec": same_y + 1 - core},
        {"occ": occ, "sec": twin_y + core},
        {"occ": occ, "sec": twin_y + 1 - core},
    )

    @pl.when(holder)
    def _():
        for t, (r0, rows) in enumerate(CHUNKS):
            settle(plane_in[t].at[pl.ds(0, 7)], p_recv.at[t])
            settle(x_out[t].at[pl.ds(0, 1)], p_send.at[t])
            total = plane_in[t][0]
            for k in range(1, 8):
                total += plane_in[t][k]
            final[r0 : r0 + rows, :] = total
        outs = [
            pltpu.make_async_remote_copy(
                src_ref=final,
                dst_ref=final,
                send_sem=f_send.at[k],
                recv_sem=f_recv,
                device_id=to,
                device_id_type=MESH,
            )
            for k, to in enumerate(group)
        ]
        for copy in outs:
            copy.start()
        for copy in outs:
            copy.wait_send()

    @pl.when(jnp.logical_not(holder))
    def _():
        for t in range(n):
            settle(x_out[t], p_send.at[t])
        settle(final, f_recv)

    turned[...] = final[...].T
    summed = turned[pl.ds(pl.multiple_of(sub * COL_SHARE, COL_SHARE), COL_SHARE), :]
    out_ref[...] = (summed + pair_ref[...]) / bottom[...] * (wide < live).astype(F32)

    for t, (r0, rows) in enumerate(CHUNKS):
        settle(send_t.at[pl.ds(0, OWNERS - 1), pl.ds(r0, rows)], t_send.at[t])
        settle(core_in[t], core_send.at[t])
        settle(y_in[t], y_send.at[t])
        settle(x_in[t], x_send.at[t])


def shards(amplitudes, live_pairs, ladder_ints, cycle_ints, pair_ints, occ_energy, vir_energy):
    n = len(CHUNKS)
    vmem = pl.BlockSpec(memory_space=pltpu.VMEM)
    hbm = pl.BlockSpec(memory_space=pltpu.HBM)
    dma = pltpu.SemaphoreType.DMA
    rows = [r for _, r in CHUNKS]
    scratch = [
        pltpu.SMEM((OWNERS,), jnp.int32),
        pltpu.SMEM((OCCUPIED,), F32),
        pltpu.SMEM((VIRTUAL,), F32),
        pltpu.VMEM((COL_SHARE, OCCUPIED), F32),
        pltpu.VMEM((X, OCCUPIED * D_SHARE, LANES), F32),
        pltpu.VMEM((A_WINDOW, DEPTH, LANES), F32),
        pltpu.VMEM((OCCUPIED * D_SHARE, J_SHARE * LANES), F32),
        pltpu.VMEM((3 * DEPTH, A_WINDOW * LANES), BF16),
        pltpu.VMEM((OWNERS * max(rows), 3 * DEPTH), BF16),
        pltpu.VMEM((OCCUPIED * D_SHARE, J_SHARE * LANES), BF16),
        pltpu.VMEM((OCCUPIED * D_SHARE, J_SHARE * LANES), BF16),
        pltpu.VMEM((OWNERS, OCCUPIED, DEPTH), F32),
        pltpu.VMEM((A_WINDOW, OCCUPIED * D_SHARE), F32),
        pltpu.VMEM((OWNERS, A_WINDOW, OCCUPIED * D_SHARE), F32),
        pltpu.VMEM((J_SHARE, OWNERS * A_WINDOW, LANES), F32),
        pltpu.VMEM((OCCUPIED, LANES), F32),
        pltpu.VMEM((LANES, OCCUPIED), F32),
        pltpu.VMEM((COL_SHARE, OCCUPIED), F32),
        dma((8,)),
        dma((4,)),
        dma((n,)),
        dma((n,)),
        dma((n,)),
        dma((n,)),
        dma((n,)),
        dma((n,)),
        dma((n,)),
        dma((n,)),
        dma((n,)),
        dma((n,)),
        dma((n,)),
        dma((3,)),
        dma,
    ]
    scratch += [pltpu.VMEM((OWNERS, r, DEPTH), F32) for r in rows]
    scratch += [pltpu.VMEM((2, 4, 2, 8 * r, LANES), F32) for r in rows]
    scratch += [pltpu.VMEM((4, 2, 8 * r, LANES), F32) for r in rows]
    scratch += [pltpu.VMEM((56 * r, LANES), F32) for r in rows]
    scratch += [pltpu.VMEM((8, r, LANES), F32) for r in rows]
    scratch += [pltpu.VMEM((X - 1, 2, r, LANES), F32) for r in rows]
    scratch += [pltpu.VMEM((2, r, LANES), F32) for r in rows]
    scratch += [pltpu.VMEM((8, r, LANES), F32) for r in rows]
    out = pl.pallas_call(
        kernel,
        out_shape=jax.ShapeDtypeStruct((COL_SHARE, OCCUPIED), F32),
        in_specs=[hbm] * 7,
        out_specs=vmem,
        scratch_shapes=scratch,
        compiler_params=pltpu.CompilerParams(
            collective_id=0, has_side_effects=True, vmem_limit_bytes=48 * 1024 * 1024
        ),
    )(
        *(
            pltpu.with_memory_space_constraint(array, pltpu.HBM)
            for array in (
                live_pairs,
                occ_energy,
                vir_energy,
                amplitudes.transpose(0, 2, 1).reshape(OCCUPIED * D_SHARE, VIRTUAL),
                ladder_ints.reshape(DEPTH, A_WINDOW * B_WINDOW),
                cycle_ints.reshape(OCCUPIED * D_SHARE, J_SHARE * B_WINDOW),
                pair_ints.T,
            )
        )
    )
    return out.T


def solution(mesh):
    in_specs = (
        P("occ", None, "sec"),
        P(),
        P("occ", "sec", None),
        P(None, "sec", "occ"),
        P("occ", "sec"),
        P(),
        P(),
    )
    return jax.shard_map(shards, mesh=mesh, in_specs=in_specs, out_specs=P("occ", "sec"), check_vma=False)
```

```python
import jax
import jax.numpy as jnp
from jax import lax
from jax.experimental import pallas as pl
from jax.experimental.pallas import tpu as pltpu
from jax.sharding import PartitionSpec as P

OCCUPIED = 48
VIRTUAL = 512
A_WINDOW = 8
B_WINDOW = 128
X = 4
Z_LOW = 4
Z_HIGH = 2
Y = 8
OWNERS = X * Z_LOW
LANES = 128
C_SHARE = VIRTUAL // OWNERS
D_SHARE = 16
DEPTH = C_SHARE * D_SHARE
J_SHARE = OCCUPIED // OWNERS
COL_SHARE = 32
CHUNKS = tuple((8 * t, 8) for t in range(6))
AHEAD = 3
MESH = pl.DeviceIdType.MESH
F32 = jnp.float32
BF16 = jnp.bfloat16


def halves(value):
    high = value.astype(BF16)
    low = (value - high.astype(F32)).astype(BF16)
    return high, low


def product(left, right):
    (lh, ll), (rh, rl) = left, right
    out = jnp.dot(lh, rl, preferred_element_type=F32)
    out += jnp.dot(ll, rh, preferred_element_type=F32)
    return out + jnp.dot(lh, rh, preferred_element_type=F32)


def settle(ref, sem):
    pltpu.make_async_copy(ref, ref, sem).wait()


def kernel(
    live_hbm, occ_hbm, vir_hbm, t_hbm, w_hbm, u_hbm, pair_hbm, out_ref,
    live_ref, occ_ref, vir_ref, pair_ref, t_v, w_v, u_v, w3, t3, uh, ul, send_t, cyc_own, cyc_all, cyc_out, final, turned, bottom,
    local_sem, cyc_sem, t_send, t_recv, core_send, core_recv, y_send, y_mid, y_recv, x_send, x_recv, p_send, p_recv,
    f_send, f_recv, *bufs,
):
    n = len(CHUNKS)
    recv_t, grid, core_in, y_in, y_out, x_in, x_out, plane_in = (
        bufs[k * n : (k + 1) * n] for k in range(8)
    )
    occ = lax.axis_index("occ")
    sec = lax.axis_index("sec")
    x, zl = occ // Z_LOW, occ % Z_LOW
    zh, y, core = sec // 16, (sec // 2) % Y, sec % 2
    half = y % 2
    slot = (occ % 2) * 8 + occ // 2
    holder = jnp.logical_and(zl % 2 == half, zh == core)

    live_copy = pltpu.make_async_copy(live_hbm, live_ref, local_sem.at[3])
    live_copy.start()
    early = CHUNKS[0][1] * D_SHARE
    late = OCCUPIED * D_SHARE - early
    def fetch_rows(part, at, size):
        for k in range(X):
            pltpu.make_async_copy(
                t_hbm.at[pl.ds(at, size), pl.ds(k * LANES, LANES)],
                t_v.at[k, pl.ds(at, size)],
                local_sem.at[7 * part],
            ).start()

    fetch_rows(0, 0, early)

    barrier = pltpu.get_barrier_semaphore()

    def greet(o, s):
        pl.semaphore_signal(barrier, inc=1, device_id={"occ": o, "sec": s}, device_id_type=MESH)

    def greet_occ(k, carry):
        greet((occ + k) % OWNERS, sec)
        return carry

    def greet_far(k, carry):
        greet(x * Z_LOW + k, (sec + 16) % 32)
        return carry

    def greet_y(k, carry):
        greet(occ, zh * 16 + ((y + k) % Y) * 2 + core)
        return carry

    lax.fori_loop(1, OWNERS, greet_occ, 0)
    lax.fori_loop(0, Z_LOW, greet_far, 0)
    lax.fori_loop(1, Y, greet_y, 0)
    y_twin = y + 1 - 2 * half
    same_y = zh * 16 + y * 2
    twin_y = zh * 16 + y_twin * 2
    greet(occ, same_y + 1 - core)
    greet(occ, twin_y + 1 - core)

    fetch_rows(1, early, late)
    for k in range(A_WINDOW):
        pltpu.make_async_copy(
            w_hbm.at[:, pl.ds(k * LANES, LANES)], w_v.at[k], local_sem.at[1]
        ).start()
    pltpu.make_async_copy(u_hbm, u_v, local_sem.at[2]).start()
    small = (
        pltpu.make_async_copy(occ_hbm, occ_ref, local_sem.at[4]),
        pltpu.make_async_copy(vir_hbm, vir_ref, local_sem.at[5]),
        pltpu.make_async_copy(pair_hbm, pair_ref, local_sem.at[6]),
    )
    for copy in small:
        copy.start()

    lane_group = lax.broadcasted_iota(jnp.int32, (8, LANES), 1) // C_SHARE
    sub_row = lax.broadcasted_iota(jnp.int32, (8, LANES), 0)

    def relay(r0, rows):
        def tile(k, carry):
            for b in range(rows // 8):
                p0 = r0 + 8 * b
                keep = sub_row + p0 < live
                for g in range(4):
                    part = [
                        jnp.where(keep, t_v[k, pl.ds(p0 * D_SHARE + 4 * g + d, 8, stride=D_SHARE), :], 0.0)
                        for d in range(4)
                    ]
                    for z in range(Z_LOW):
                        row = None
                        for d in range(4):
                            shift = ((d - z) * C_SHARE) % LANES
                            turn = pltpu.roll(part[d], shift, 1) if shift else part[d]
                            row = turn if row is None else jnp.where(lane_group == d, turn, row)
                        send_t[k * Z_LOW + z, p0 : p0 + 8, g * LANES : (g + 1) * LANES] = row
            return carry

        lax.fori_loop(0, X, tile, 0)

    def send_rows(t):
        r0, rows = CHUNKS[t]

        def one(k, carry):
            o = (occ + k) % OWNERS
            pltpu.make_async_remote_copy(
                src_ref=send_t.at[o, pl.ds(r0, rows)],
                dst_ref=recv_t[t].at[slot],
                send_sem=t_send.at[t],
                recv_sem=t_recv.at[t],
                device_id={"occ": o, "sec": sec},
                device_id_type=MESH,
            ).start()
            return carry

        lax.fori_loop(1, OWNERS, one, 0)
        recv_t[t][slot] = send_t[occ, r0 : r0 + rows, :]

    live_copy.wait()
    live = live_ref[occ]
    settle(t_v.at[:, pl.ds(0, early)], local_sem.at[0])
    relay(*CHUNKS[0])
    pl.semaphore_wait(barrier, 28)
    send_rows(0)
    settle(t_v.at[:, pl.ds(early, late)], local_sem.at[7])
    for q in range(OCCUPIED * D_SHARE // LANES):
        rows = lax.broadcasted_iota(jnp.int32, (LANES, LANES), 0) // D_SHARE + q * (LANES // D_SHARE)
        block = jnp.where(rows < live, t_v[0, q * LANES : (q + 1) * LANES, :], 0.0)
        cyc_own[:, q * LANES : (q + 1) * LANES] = block.T[:A_WINDOW, :]

    def cyc_z(k, carry):
        pltpu.make_async_remote_copy(
            src_ref=cyc_own,
            dst_ref=cyc_all.at[occ],
            send_sem=cyc_sem.at[0],
            recv_sem=cyc_sem.at[1],
            device_id={"occ": x * Z_LOW + (zl + k) % Z_LOW, "sec": sec},
            device_id_type=MESH,
        ).start()
        return carry

    lax.fori_loop(1, Z_LOW, cyc_z, 0)
    cyc_all[occ] = cyc_own[...]
    for t in range(1, AHEAD):
        relay(*CHUNKS[t])
        send_rows(t)

    settle(cyc_all.at[pl.ds(0, Z_LOW - 1)], cyc_sem.at[1])

    def cyc_x(k, carry):
        mine = cyc_all.at[pl.ds(x * Z_LOW, Z_LOW)]
        pltpu.make_async_remote_copy(
            src_ref=mine,
            dst_ref=mine,
            send_sem=cyc_sem.at[2],
            recv_sem=cyc_sem.at[3],
            device_id={"occ": ((x + k) % X) * Z_LOW + zl, "sec": sec},
            device_id_type=MESH,
        ).start()
        return carry

    lax.fori_loop(1, X, cyc_x, 0)
    settle(w_v, local_sem.at[1])

    def weights(a, carry):
        col = pl.multiple_of(((a % 4) * 2 + a // 4) * LANES, LANES)
        for d in range(D_SHARE):
            high, low = halves(w_v[a, pl.ds(d, C_SHARE, stride=D_SHARE), :])
            for k, half_of in enumerate((low, high, high)):
                w3[k * DEPTH + d * C_SHARE : k * DEPTH + (d + 1) * C_SHARE, pl.ds(col, LANES)] = half_of
        return carry

    lax.fori_loop(0, A_WINDOW, weights, 0)
    settle(u_v, local_sem.at[2])
    for k in range(0, OCCUPIED * D_SHARE, LANES):
        uh[k : k + LANES, :], ul[k : k + LANES, :] = halves(u_v[k : k + LANES, :])

    settle(cyc_all.at[pl.ds(0, OWNERS - Z_LOW)], cyc_sem.at[3])
    settle(cyc_all.at[pl.ds(0, Z_LOW - 1)], cyc_sem.at[0])
    settle(cyc_all.at[pl.ds(0, OWNERS - Z_LOW)], cyc_sem.at[2])
    rows_cyc = halves(cyc_all[...].reshape(OWNERS * A_WINDOW, OCCUPIED * D_SHARE))
    cyc = product(rows_cyc, (uh[...], ul[...]))
    for jj in range(J_SHARE):
        cyc_out[jj] = cyc[:, jj * LANES : (jj + 1) * LANES]

    wide = lax.broadcasted_iota(jnp.int32, (COL_SHARE, OCCUPIED), 1)
    tall = lax.broadcasted_iota(jnp.int32, (COL_SHARE, OCCUPIED), 0)
    sub = half * 2 + core

    def denominators():
        for copy in small:
            copy.wait()
        occ_pair = lax.fori_loop(
            0, OCCUPIED, lambda j, v: jnp.where(wide == j, occ_ref[occ] + occ_ref[j], v),
            jnp.zeros((COL_SHARE, OCCUPIED), F32),
        )
        vir_pair = lax.fori_loop(
            0, COL_SHARE,
            lambda b, v: jnp.where(tall == b, vir_ref[zh * 4 + y // 2] + vir_ref[sub * COL_SHARE + b], v),
            jnp.zeros((COL_SHARE, OCCUPIED), F32),
        )
        bottom[...] = occ_pair - vir_pair

    def core_piece(t, al):
        return pltpu.make_async_remote_copy(
            src_ref=grid[t].at[1 - core, al],
            dst_ref=core_in[t].at[al],
            send_sem=core_send.at[t],
            recv_sem=core_recv.at[t],
            device_id={"occ": occ, "sec": same_y + 1 - core},
            device_id_type=MESH,
        )

    def ladder(t):
        settle(recv_t[t].at[pl.ds(0, OWNERS - 1)], t_recv.at[t])
        r0, rows = CHUNKS[t]
        if t + AHEAD < n:
            relay(*CHUNKS[t + AHEAD])
            send_rows(t + AHEAD)
        high, low = halves(recv_t[t][...].reshape(OWNERS * rows, DEPTH))
        left = t3.at[pl.ds(0, OWNERS * rows)]
        left[:, :DEPTH] = high
        left[:, DEPTH : 2 * DEPTH] = low
        left[:, 2 * DEPTH :] = high
        for al in range(4):
            if al % 2 == 0:
                cols = slice(al * 2 * LANES, (al + 2) * 2 * LANES)
                out = 0.5 * jnp.dot(left[...], w3[:, cols], preferred_element_type=F32)
                for q in range(4):
                    piece = out[:, q * LANES : (q + 1) * LANES]
                    grid[t][q % 2, al + q // 2] = piece.reshape(2, 8 * rows, LANES)
            for jj in range(J_SHARE):
                row = occ * J_SHARE + jj - r0

                @pl.when(jnp.logical_and(row >= 0, row < rows))
                def _():
                    for ah in range(2):
                        for e in range(2):
                            here = (ah, al, e, pl.ds(row, 8, stride=rows), slice(None))
                            a = ah * 4 + al
                            grid[t][here] += cyc_out[jj, pl.ds(e * A_WINDOW + a, 8, stride=2 * A_WINDOW), :]

            core_piece(t, al).start()

    def ship(src, dst, send, recv, to):
        pltpu.make_async_remote_copy(
            src_ref=src,
            dst_ref=dst,
            send_sem=send,
            recv_sem=recv,
            device_id={"occ": occ, "sec": zh * 16 + to * 2 + core},
            device_id_type=MESH,
        ).start()

    def portion(t, to):
        return grid[t].at[core, to // 2, to % 2]

    steps = ((0, 1), (1, Y - 1))

    def first_round(t):
        settle(core_in[t], core_recv.at[t])
        grid[t][core] += core_in[t][...]
        part = 4 * CHUNKS[t][1]
        for d, step in steps:
            ship(
                portion(t, (y + 3 * step) % Y), y_in[t].at[pl.ds(d * 2 * part, 2 * part)],
                y_send.at[t], y_mid.at[t], (y + step) % Y,
            )
            ship(
                portion(t, (y + 4) % Y).at[pl.ds(d * part, part)], y_in[t].at[pl.ds((4 + d) * part, part)],
                y_send.at[t], y_mid.at[t], (y + 2 * step) % Y,
            )
        for d, step in steps:
            ship(
                portion(t, (y + step) % Y), y_in[t].at[pl.ds((6 + 2 * d) * part, 2 * part)],
                y_send.at[t], y_recv.at[t], (y + step) % Y,
            )

    def second_round(t):
        part = 4 * CHUNKS[t][1]
        settle(y_in[t].at[pl.ds(0, 6 * part)], y_mid.at[t])
        for d, step in steps:
            to = (y + 2 * step) % Y
            whole = portion(t, to)
            whole[...] += y_in[t][d * 2 * part : (d + 1) * 2 * part, :]
            whole[d * part : (d + 1) * part, :] += y_in[t][(4 + d) * part : (5 + d) * part, :]
            ship(
                whole, y_in[t].at[pl.ds((10 + 2 * d) * part, 2 * part)],
                y_send.at[t], y_recv.at[t], to,
            )

    def along_x(t):
        r0, rows = CHUNKS[t]
        part = 4 * rows
        settle(y_in[t].at[pl.ds(6 * part, 8 * part)], y_recv.at[t])
        total = grid[t][core, y // 2, half]
        for k in range(4):
            total += y_in[t][(6 + 2 * k) * part : (8 + 2 * k) * part, :]
        y_out[t][...] = total.reshape(8, rows, LANES)

        for k in range(1, X):
            to = (x + k) % X
            pltpu.make_async_remote_copy(
                src_ref=y_out[t].at[pl.ds(2 * to, 2)],
                dst_ref=x_in[t].at[k - 1],
                send_sem=x_send.at[t],
                recv_sem=x_recv.at[t],
                device_id={"occ": to * Z_LOW + zl, "sec": sec},
                device_id_type=MESH,
            ).start()

    def along_z(t):
        settle(x_in[t], x_recv.at[t])
        total = y_out[t][pl.ds(2 * x, 2)]
        for k in range(X - 1):
            total += x_in[t][k]
        x_out[t][...] = total
        for k in range(2):
            mine = jnp.logical_and(holder, zl // 2 == k)

            @pl.when(jnp.logical_not(mine))
            def _():
                pltpu.make_async_remote_copy(
                    src_ref=x_out[t].at[k],
                    dst_ref=plane_in[t].at[zh * Z_LOW + zl],
                    send_sem=p_send.at[t],
                    recv_sem=p_recv.at[t],
                    device_id={"occ": x * Z_LOW + 2 * k + half, "sec": core * 16 + y * 2 + core},
                    device_id_type=MESH,
                ).start()

            @pl.when(mine)
            def _():
                plane_in[t][zh * Z_LOW + zl] = x_out[t][k]

    group = (
        {"occ": occ, "sec": same_y + 1 - core},
        {"occ": occ, "sec": twin_y + core},
        {"occ": occ, "sec": twin_y + 1 - core},
    )

    def share(t):
        @pl.when(holder)
        def _():
            r0, rows = CHUNKS[t]
            settle(plane_in[t].at[pl.ds(0, 7)], p_recv.at[t])
            total = plane_in[t][0]
            for k in range(1, 8):
                total += plane_in[t][k]
            final[r0 : r0 + rows, :] = total
            for k, to in enumerate(group):
                piece = final.at[pl.ds(r0, rows)]
                pltpu.make_async_remote_copy(
                    src_ref=piece, dst_ref=piece, send_sem=f_send.at[k], recv_sem=f_recv,
                    device_id=to, device_id_type=MESH,
                ).start()

    for t in range(n + 4):
        if t < n:
            ladder(t)
            first_round(t)
        if 0 <= t - 5:
            share(t - 5)
        if 0 <= t - 4:
            along_z(t - 4)
        if 0 <= t - 3 < n:
            along_x(t - 3)
        if 0 <= t - 1 < n:
            second_round(t - 1)
        if t == 0:
            denominators()
    share(n - 1)

    @pl.when(jnp.logical_not(holder))
    def _():
        settle(final, f_recv)

    turned[...] = final[...].T
    summed = turned[pl.ds(pl.multiple_of(sub * COL_SHARE, COL_SHARE), COL_SHARE), :]
    out_ref[...] = (summed + pair_ref[...]) / bottom[...] * (wide < live).astype(F32)

    for t, (r0, rows) in enumerate(CHUNKS):
        settle(send_t.at[pl.ds(0, OWNERS - 1), pl.ds(r0, rows)], t_send.at[t])
        settle(core_in[t], core_send.at[t])
        settle(y_in[t], y_send.at[t])
        settle(x_in[t], x_send.at[t])
        @pl.when(holder)
        def _():
            settle(x_out[t].at[pl.ds(0, 1)], p_send.at[t])

        @pl.when(jnp.logical_not(holder))
        def _():
            settle(x_out[t], p_send.at[t])

    @pl.when(holder)
    def _():
        for k in range(3):
            settle(final, f_send.at[k])


def shards(amplitudes, live_pairs, ladder_ints, cycle_ints, pair_ints, occ_energy, vir_energy):
    n = len(CHUNKS)
    vmem = pl.BlockSpec(memory_space=pltpu.VMEM)
    hbm = pl.BlockSpec(memory_space=pltpu.HBM)
    dma = pltpu.SemaphoreType.DMA
    rows = [r for _, r in CHUNKS]
    scratch = [
        pltpu.SMEM((OWNERS,), jnp.int32),
        pltpu.SMEM((OCCUPIED,), F32),
        pltpu.SMEM((VIRTUAL,), F32),
        pltpu.VMEM((COL_SHARE, OCCUPIED), F32),
        pltpu.VMEM((X, OCCUPIED * D_SHARE, LANES), F32),
        pltpu.VMEM((A_WINDOW, DEPTH, LANES), F32),
        pltpu.VMEM((OCCUPIED * D_SHARE, J_SHARE * LANES), F32),
        pltpu.VMEM((3 * DEPTH, A_WINDOW * LANES), BF16),
        pltpu.VMEM((OWNERS * max(rows), 3 * DEPTH), BF16),
        pltpu.VMEM((OCCUPIED * D_SHARE, J_SHARE * LANES), BF16),
        pltpu.VMEM((OCCUPIED * D_SHARE, J_SHARE * LANES), BF16),
        pltpu.VMEM((OWNERS, OCCUPIED, DEPTH), F32),
        pltpu.VMEM((A_WINDOW, OCCUPIED * D_SHARE), F32),
        pltpu.VMEM((OWNERS, A_WINDOW, OCCUPIED * D_SHARE), F32),
        pltpu.VMEM((J_SHARE, OWNERS * A_WINDOW, LANES), F32),
        pltpu.VMEM((OCCUPIED, LANES), F32),
        pltpu.VMEM((LANES, OCCUPIED), F32),
        pltpu.VMEM((COL_SHARE, OCCUPIED), F32),
        dma((8,)),
        dma((4,)),
        dma((n,)),
        dma((n,)),
        dma((n,)),
        dma((n,)),
        dma((n,)),
        dma((n,)),
        dma((n,)),
        dma((n,)),
        dma((n,)),
        dma((n,)),
        dma((n,)),
        dma((3,)),
        dma,
    ]
    scratch += [pltpu.VMEM((OWNERS, r, DEPTH), F32) for r in rows]
    scratch += [pltpu.VMEM((2, 4, 2, 8 * r, LANES), F32) for r in rows]
    scratch += [pltpu.VMEM((4, 2, 8 * r, LANES), F32) for r in rows]
    scratch += [pltpu.VMEM((56 * r, LANES), F32) for r in rows]
    scratch += [pltpu.VMEM((8, r, LANES), F32) for r in rows]
    scratch += [pltpu.VMEM((X - 1, 2, r, LANES), F32) for r in rows]
    scratch += [pltpu.VMEM((2, r, LANES), F32) for r in rows]
    scratch += [pltpu.VMEM((8, r, LANES), F32) for r in rows]
    out = pl.pallas_call(
        kernel,
        out_shape=jax.ShapeDtypeStruct((COL_SHARE, OCCUPIED), F32),
        in_specs=[hbm] * 7,
        out_specs=vmem,
        scratch_shapes=scratch,
        compiler_params=pltpu.CompilerParams(
            collective_id=0, has_side_effects=True, vmem_limit_bytes=48 * 1024 * 1024
        ),
    )(
        *(
            pltpu.with_memory_space_constraint(array, pltpu.HBM)
            for array in (
                live_pairs,
                occ_energy,
                vir_energy,
                amplitudes.transpose(0, 2, 1).reshape(OCCUPIED * D_SHARE, VIRTUAL),
                ladder_ints.reshape(DEPTH, A_WINDOW * B_WINDOW),
                cycle_ints.reshape(OCCUPIED * D_SHARE, J_SHARE * B_WINDOW),
                pair_ints.T,
            )
        )
    )
    return out.T


def solution(mesh):
    in_specs = (
        P("occ", None, "sec"),
        P(),
        P("occ", "sec", None),
        P(None, "sec", "occ"),
        P("occ", "sec"),
        P(),
        P(),
    )
    return jax.shard_map(shards, mesh=mesh, in_specs=in_specs, out_specs=P("occ", "sec"), check_vma=False)
```
